32 devices in a mesh: lon: 2 (over x), lat: 4 (over z), mem: 4 (over y, core).
Axes of the slice: x: 2, y: 2, z: 4, core: 2. Of those that a mesh axis runs over, the one named last changes fastest.
Arguments:
- tracer: float32 [128, 8, 32, 256], P('mem', None, 'lat', 'lon'), parts along dimension 0, may hold values from -3 to 3
- courant: float32 [2, 8, 32, 256], P(None, None, 'lat', 'lon'), may hold values from -0.45 to 0.45
- mixing: float32 [7, 32, 256], P(None, 'lat', 'lon'), may hold values from 0.1 to 10
- forcing: float32 [5, 24576], P(None, ('lon', 'lat')), may hold values from 0 to 1
- plant_type: int32 [24576], P(('lon', 'lat')), may hold values from 0 to 15
- land_params: float32 [3, 128, 16], P(None, 'mem'), parts along dimension 1, may hold values from 0 to 1
- send_slot: int32 [24576], P(('lon', 'lat')), may hold values from -1 to 4095, as said below
- recv_cell: int32 [64, 512], P(('lon', 'lat')), may hold values from 0 to 1024, as said below
Outputs:
- tracer_next: float32 [128, 8, 32, 256], P('mem', None, 'lat', 'lon'), parts along dimension 0
- surface_flux: float32 [128, 32, 256], P('mem', 'lat', 'lon'), parts along dimension 0
The draws below stay inside these ranges and needn't reach their ends.
There are 4 independent parts, one for each index of `mem`. The reference program is written for one: setup_inputs(seed, part) draws one part's arguments, and reference() takes and returns one part's arrays. A program takes and returns all parts, laid end to end along the dimension named above; an argument that names none is the same for every part. Nothing has to cross between parts.
Inputs may be any that keep to these rules, and one draw needn't show every extreme that they name: `send_slot`: -1 marks an empty column slot; otherwise the value is tile * 512 + place. Each device holds 1536 or more live columns and some device holds 3072. No two columns of one device share a tile and place, at most 512 columns of one device go to one tile, and that many are reached. A quarter of the tiles receive no columns. `recv_cell`: row t * 8 + d, place k gives the local cell (row * 128 + column) of tile t for the column that device d sends to that place, or 1024 where it sends none; it agrees with send_slot.
All inputs are finite; a program needn't handle non-finite values.
Results may differ from the reference program's by a relative error of at most 0.0003.
Values sent between devices are 32-bit elements; how exact they have to be, the bound alone decides.
A program may use at most 64 MiB of HBM per device.

```python
import math
import jax
import jax.numpy as jnp
from jax import lax

MEMB = 32
LEV = 8
PFT = 16
TX = 128
TY = 8
CAP = 3072
TILES = 8
LAND_TILES = 6
SLOT = 512
NX = 256
NY = 32
COLS = 24576
N_LAT = 4


def coupling_tables(key):
    base_key = jax.random.fold_in(key, 4099)
    key_live, key_land, key_order, key_place, key_cell, key_full = jax.random.split(base_key, 6)
    device_ids = jnp.arange(TILES, dtype=jnp.int32)
    live_count = jax.random.randint(key_live, (TILES,), CAP // 2, CAP + 1)
    full_device = jax.random.randint(key_full, (), 0, TILES)
    live_count = jnp.where(device_ids == full_device, CAP, live_count)
    land_list = jax.random.permutation(key_land, TILES)[:LAND_TILES]
    orders = jax.vmap(lambda entry_key: jax.random.permutation(entry_key, LAND_TILES))(jax.random.split(key_order, TILES))
    destination = land_list[orders]
    places = jax.vmap(lambda entry_key: jax.random.permutation(entry_key, CAP))(jax.random.split(key_place, TILES))
    column_ids = jnp.arange(CAP, dtype=jnp.int32)
    target_tile = destination[:, column_ids % LAND_TILES]
    slot_value = target_tile * SLOT + column_ids[None, :] // LAND_TILES
    slot_value = jnp.where(column_ids[None, :] < live_count[:, None], slot_value, -1).astype(jnp.int32)
    send_table = jnp.zeros((TILES, CAP), jnp.int32).at[device_ids[:, None], places].set(slot_value)
    rank_values = jnp.broadcast_to(jnp.arange(LAND_TILES, dtype=jnp.int32)[None, :], (TILES, LAND_TILES))
    rank_table = jnp.full((TILES, TILES), CAP + 1, jnp.int32).at[device_ids[:, None], destination].set(rank_values)
    slot_ids = jnp.arange(SLOT, dtype=jnp.int32)
    slot_used = slot_ids[None, None, :] * LAND_TILES + rank_table.T[:, :, None] < live_count[None, :, None]
    cell_draw = jax.random.randint(key_cell, (TILES, TILES, SLOT), 0, TY * TX)
    recv_table = jnp.where(slot_used, cell_draw, TY * TX).astype(jnp.int32).reshape(TILES * TILES, SLOT)
    return (send_table.reshape(TILES * CAP), recv_table)


def draw_send_slot(key, part):
    return coupling_tables(key)[0]


def draw_recv_cell(key, part):
    return coupling_tables(key)[1]


def set_ends(values, own_key, smallest, largest):
    dims = values.shape
    spot = [jax.random.randint(jax.random.fold_in(own_key, axis), (), 0, dims[axis]) for axis in range(len(dims))]
    values = values.at[tuple(spot)].set(smallest)
    longest = dims.index(max(dims))
    spot[longest] = (spot[longest] + 1) % dims[longest]
    return values.at[tuple(spot)].set(largest)


def level_of(own_key, shape, cuts, smallest, top_value):
    gain = 1.0
    for dim, parts in cuts:
        draws = jax.random.uniform(jax.random.fold_in(jax.random.fold_in(own_key, 6), dim), (parts,), jnp.float32, smallest / len(cuts), top_value / len(cuts))
        gain = gain * jnp.repeat(jnp.exp(draws), shape[dim] // parts).reshape((-1,) + (1,) * (len(shape) - 1 - dim))
    return gain


def centred(rng, shape, deviation, most, cuts=(), kind=jnp.bfloat16):
    entries = jax.random.normal(rng, shape, jnp.float32) * deviation
    if len(cuts) > 0:
        entries = level_of(rng, shape, cuts, -0.22, 0.18) * entries
    return jnp.clip(entries, min=-most, max=most).astype(kind)


def setup_inputs(seed: int = 0, part: int = 0) -> dict:
    keys = jax.random.split(jax.random.key(seed), 9)
    part_keys = jax.random.split(jax.random.fold_in(keys[8], part), 9)
    return {
        "tracer": centred(part_keys[0], (MEMB, LEV, NY, NX), 1.0, 3.0, ((2, 4), (3, 2)), jnp.float32),
        "courant": jnp.clip(jax.random.uniform(keys[1], (2, LEV, NY, NX), jnp.float32, -0.45, 0.45) * level_of(keys[1], (2, LEV, NY, NX), ((2, 4), (3, 2)), -0.4, 0.0), -0.45, 0.45),
        "mixing": jnp.clip(jnp.exp(math.log(10.0) - 4.6051702 * jax.random.uniform(keys[2], (LEV - 1, NY, NX), jnp.float32) ** level_of(keys[2], (LEV - 1, NY, NX), ((1, 4), (2, 2)), -0.2, 0.2)), 0.1, 10.0),
        "forcing": jnp.clip(1.0 * jax.random.uniform(keys[3], (5, COLS), jnp.float32) ** level_of(keys[3], (5, COLS), ((1, 8),), -0.2, 0.2), 0.0, 1.0),
        "plant_type": set_ends(jax.random.randint(keys[4], (COLS,), 0, PFT), jax.random.fold_in(keys[4], 1), 0, PFT - 1).astype(jnp.int32),
        "land_params": jnp.clip(jax.random.uniform(part_keys[5], (3, MEMB, PFT), jnp.float32, 0.0, 1.0), 0.0, 1.0),
        "send_slot": draw_send_slot(jax.random.fold_in(keys[8], 71), part),
        "recv_cell": draw_recv_cell(jax.random.fold_in(keys[8], 71), part),
    }


FLUX_SCALE = 0.02
GAS_CONSTANT = 8.314

def arrhenius(energy, leaf_temp):
    return jnp.exp(energy * (leaf_temp - 25.0) / (298.15 * GAS_CONSTANT * (leaf_temp + 273.15)))

def column_exchange(drivers, param_rows, bottom_tracer):
    light = 2000.0 * drivers[0]
    leaf_temp = 35.0 * drivers[1]
    water_factor = 0.2 + 0.8 * drivers[2]
    leaf_area = 0.5 + 5.5 * drivers[3]
    area_share = 0.05 + 0.55 * drivers[4]
    carbox_ref = 30.0 + 70.0 * param_rows[0]
    transport_ratio = 1.4 + 0.8 * param_rows[1]
    respiration_share = 0.005 + 0.025 * param_rows[2]
    carbon_leaf = 0.7 * (400.0 + 100.0 * bottom_tracer)
    carboxylation = carbox_ref * arrhenius(65330.0, leaf_temp) * water_factor
    transport_max = transport_ratio * carbox_ref * arrhenius(43540.0, leaf_temp)
    michaelis_carbon = 404.9 * arrhenius(79430.0, leaf_temp)
    michaelis_oxygen = 278.4 * arrhenius(36380.0, leaf_temp)
    compensation = 42.75 * arrhenius(37830.0, leaf_temp)
    absorbed = 0.425 * light
    total_rate = absorbed + transport_max
    electron_rate = (total_rate - jnp.sqrt(total_rate * total_rate - 2.8 * absorbed * transport_max)) / 1.4
    rubisco_rate = carboxylation * (carbon_leaf - compensation) / (carbon_leaf + michaelis_carbon * (1.0 + 210.0 / michaelis_oxygen))
    light_rate = electron_rate * (carbon_leaf - compensation) / (4.0 * carbon_leaf + 8.0 * compensation)
    gross_rate = jnp.minimum(rubisco_rate, light_rate)
    canopy_scale = (1.0 - jnp.exp(-0.5 * leaf_area)) / 0.5
    return -FLUX_SCALE * area_share * canopy_scale * (gross_rate - respiration_share * carboxylation)

def window(array_in, start_at, count, dimension):
    return lax.slice_in_dim(array_in, start_at, start_at + count, axis=dimension)

def flux_divergence(padded, courant_pad, dimension):
    extent = padded.shape[dimension] - 6
    edge_values = 7.0 / 12.0 * (window(padded, 1, extent + 3, dimension) + window(padded, 2, extent + 3, dimension)) - 1.0 / 12.0 * (window(padded, 0, extent + 3, dimension) + window(padded, 3, extent + 3, dimension))
    left_low = window(edge_values, 0, extent + 1, dimension)
    left_high = window(edge_values, 1, extent + 1, dimension)
    right_high = window(edge_values, 2, extent + 1, dimension)
    left_mean = window(padded, 2, extent + 1, dimension)
    right_mean = window(padded, 3, extent + 1, dimension)
    face_courant = window(courant_pad, 2, extent + 1, dimension)
    slope_left = left_high - left_low
    curve_left = 6.0 * (left_mean - 0.5 * (left_low + left_high))
    slope_right = right_high - left_high
    curve_right = 6.0 * (right_mean - 0.5 * (left_high + right_high))
    from_left = left_high - 0.5 * face_courant * (slope_left - (1.0 - 2.0 / 3.0 * face_courant) * curve_left)
    from_right = left_high - 0.5 * face_courant * (slope_right + (1.0 + 2.0 / 3.0 * face_courant) * curve_right)
    fluxes = face_courant * jnp.where(face_courant > 0, from_left, from_right)
    return window(fluxes, 1, extent, dimension) - window(fluxes, 0, extent, dimension)

def implicit_mixing(rhs_field, coefficient):
    layers = rhs_field.shape[-3]
    ratios = []
    sweep_values = []
    for layer_index in range(layers):
        weight_below = coefficient[layer_index - 1] if layer_index > 0 else jnp.zeros_like(coefficient[0])
        weight_above = coefficient[layer_index] if layer_index < layers - 1 else jnp.zeros_like(coefficient[0])
        pivot_value = 1.0 + weight_below + weight_above
        carried = rhs_field[..., layer_index, :, :]
        if layer_index > 0:
            pivot_value = pivot_value - weight_below * ratios[-1]
            carried = carried + weight_below * sweep_values[-1]
        ratios.append(weight_above / pivot_value)
        sweep_values.append(carried / pivot_value)
    solved = [sweep_values[-1]]
    for layer_index in range(layers - 2, -1, -1):
        solved.insert(0, sweep_values[layer_index] + ratios[layer_index] * solved[0])
    return jnp.stack(solved, axis=-3)

def reference(tracer, courant, mixing, forcing, plant_type, land_params, send_slot, recv_cell):
    live_column = send_slot >= 0
    target_tile = jnp.where(live_column, send_slot // SLOT, 0).astype(jnp.int32)
    target_place = jnp.where(live_column, send_slot % SLOT, 0).astype(jnp.int32)
    source_device = (jnp.arange(COLS, dtype=jnp.int32) // CAP).astype(jnp.int32)
    local_cell = recv_cell[target_tile * TILES + source_device, target_place]
    grid_row = target_tile % N_LAT * TY + local_cell // TX
    grid_column = target_tile // N_LAT * TX + local_cell % TX
    flat_cell = jnp.where(live_column, grid_row * NX + grid_column, NY * NX).astype(jnp.int32)
    bottom = tracer[:, 0].reshape(MEMB, NY * NX)
    bottom_tracer = jnp.take(bottom, jnp.minimum(flat_cell, NY * NX - 1), axis=1)
    param_rows = land_params[:, :, plant_type]
    column_flux = column_exchange(forcing, param_rows, bottom_tracer)
    surface = jnp.zeros((MEMB, NY * NX), jnp.float32).at[:, flat_cell].add(column_flux, mode='drop')
    surface = surface.reshape(MEMB, NY, NX)
    wind_east = courant[0]
    row_ids = lax.broadcasted_iota(jnp.int32, (1, NY, 1), 1)
    wind_north = jnp.where(row_ids == NY - 1, 0.0, courant[1])
    wind_east_pad = jnp.pad(wind_east, ((0, 0), (0, 0), (3, 3)), mode='wrap')
    wind_north_pad = jnp.pad(wind_north, ((0, 0), (3, 3), (0, 0)))

    def member_step(operands):
        member_tracer, member_surface = operands
        east_pad = jnp.pad(member_tracer, ((0, 0), (0, 0), (3, 3)), mode='wrap')
        north_pad = jnp.pad(member_tracer, ((0, 0), (3, 3), (0, 0)))
        advected = member_tracer - flux_divergence(east_pad, wind_east_pad, 2) - flux_divergence(north_pad, wind_north_pad, 1)
        forced = advected.at[0].add(member_surface)
        return implicit_mixing(forced, mixing)
    tracer_next = lax.map(member_step, (tracer, surface))
    return (tracer_next, surface)
```

```python
import functools

import jax
import jax.numpy as jnp
from jax import lax
from jax.experimental import pallas as pl
from jax.experimental.pallas import tpu as pltpu
from jax.sharding import PartitionSpec as P

FLUX_SCALE = 0.02
GAS_CONSTANT = 8.314
LANES = 128
ROWS = 8
GROUPS = 8
NT = (((1,), (1,)), ((), ()))


def iota(shape, dim):
    return lax.broadcasted_iota(jnp.int32, shape, dim)


def face_weights(c):
    size = jnp.abs(c) * 0.5
    slope = size * (1.0 - 2.0 / 3.0 * jnp.abs(c))
    edge = c * (1.0 - size - 3.0 * slope)
    far = c * (size - 3.0 * slope)
    mean = 6.0 * c * slope
    left = c > 0
    beta = jnp.where(left, far, 0.0)
    gamma = jnp.where(left, 0.0, far)
    delta = jnp.where(left, mean, 0.0)
    eps = jnp.where(left, 0.0, mean)
    a, b = 7.0 / 12.0, 1.0 / 12.0
    return [
        -b * beta,
        a * beta - b * edge,
        a * edge + a * beta - b * gamma + delta,
        a * edge - b * beta + a * gamma + eps,
        a * gamma - b * edge,
        -b * gamma,
    ]


def stencil(after, before):
    zero = jnp.zeros_like(after)
    high, low = face_weights(after), face_weights(before)
    return [
        (low[k] if k < 6 else zero) - (high[k - 1] if k > 0 else zero) for k in range(7)
    ]


def arrhenius(energy, leaf_temp):
    return jnp.exp(energy * (leaf_temp - 25.0) / (298.15 * GAS_CONSTANT * (leaf_temp + 273.15)))


def lane_take(table, index):
    return jnp.take_along_axis(table, index, axis=1, mode="promise_in_bounds")


def flip(value, k, count):
    result, bit = 0, 1
    while bit < count:
        result = result + (value // bit + k // bit) % 2 * bit
        bit *= 2
    return result


def pack_columns(stride, forcing_ref, plant_ref, slot_ref, out_ref, values_ref):
    columns = slot_ref.shape[1]
    tall = values_ref.shape[0]
    turns = tall // stride
    for t in range(turns):
        values_ref[t * stride : t * stride + 5, :] = forcing_ref[...]
        values_ref[t * stride + 5 : t * stride + 6, :] = plant_ref[...].astype(jnp.float32)
        if stride > 6:
            values_ref[t * stride + 6 : (t + 1) * stride, :] = jnp.zeros(
                (stride - 6, columns), jnp.float32
            )
    step = 512
    turn = iota((tall, step), 0) // stride
    total = jnp.zeros(out_ref.shape, jnp.float32)
    for start in range(0, columns, step):
        slot = slot_ref[:, start : start + step]
        chunk = jnp.broadcast_to(slot >> 7, (tall, step)) - turn
        lane = jnp.broadcast_to(slot & 127, (LANES, step))
        onehot = jnp.where(iota((LANES, step), 0) == lane, 1.0, 0.0).astype(jnp.bfloat16)
        rest = values_ref[:, start : start + step]
        for _ in range(3):
            piece = rest.astype(jnp.bfloat16).astype(jnp.float32)
            rest = rest - piece
            spread = jnp.concatenate(
                [
                    jnp.where(chunk == h * turns, piece, 0.0)
                    for h in range(out_ref.shape[0] // tall)
                ],
                axis=0,
            ).astype(jnp.bfloat16)
            total = total + lax.dot_general(
                spread, onehot, NT, preferred_element_type=jnp.float32
            )
    out_ref[...] = total


def pack_rows(tracer_ref, courant_ref, north_ref, south_ref, tip_ref):
    fields = tracer_ref.shape[0] // ROWS - 2
    levels = courant_ref.shape[0] // (2 * ROWS)
    part = fields // GROUPS
    for g in range(GROUPS):
        first = ROWS + g * part * ROWS
        for k in range(3):
            at = slice((g * 3 + k) * part, (g * 3 + k + 1) * part)
            north_ref[at, :] = tracer_ref[pl.ds(first + ROWS - 3 + k, part, stride=ROWS), :]
            south_ref[at, :] = tracer_ref[pl.ds(first + k, part, stride=ROWS), :]
    tip_ref[...] = courant_ref[pl.ds(levels * ROWS + ROWS - 1, levels, stride=ROWS), :]


def pack_lanes(tracer_ref, courant_ref, ends_ref):
    fields = tracer_ref.shape[0] // ROWS - 2
    levels = courant_ref.shape[0] // (2 * ROWS)
    slot = iota((ROWS, LANES), 1) >> 3

    def pack(source_ref, first, count):
        packed = jnp.zeros((ROWS, LANES), jnp.float32)
        for i in range(count):
            cells = source_ref[pl.ds(pl.multiple_of(first + i * ROWS, ROWS), ROWS), :]
            packed = jnp.where(slot == i, pltpu.roll(cells, 3 + 8 * i, 1), packed)
        return packed

    def group(j, carry):
        ends_ref[pl.ds(pl.multiple_of(j * ROWS, ROWS), ROWS), :] = pack(
            tracer_ref, ROWS + j * 16 * ROWS, 16
        )
        return carry

    lax.fori_loop(0, fields // 16, group, 0)
    last = fields // 16 * ROWS
    ends_ref[last : last + ROWS, :] = pack(courant_ref, 0, levels)


def prepare_exchange(tracer_ref, params_ref, cell_ref, bottom_ref, sum_ref, table_ref, cells_ref):
    members = params_ref.shape[2]
    tall = (tracer_ref.shape[0] - 2 * ROWS) // members
    per_row = cell_ref.shape[1] // LANES
    for j in range(per_row):
        if per_row > 1:
            cells_ref[pl.ds(j, cell_ref.shape[0], stride=per_row), :] = cell_ref[
                :, j * LANES : (j + 1) * LANES
            ]
        else:
            cells_ref[...] = cell_ref[...]
    types = params_ref.shape[1]
    for v, (low, span) in enumerate([(30.0, 70.0), (1.4, 0.8), (0.005, 0.025)]):
        sum_ref[:LANES, :] = jnp.zeros((LANES, LANES), jnp.float32)
        sum_ref[:types, :members] = params_ref[v]
        table_ref[v] = low + span * sum_ref[:LANES, :].T[:members, :]
    for r in range(ROWS):
        bottom_ref[r] = tracer_ref[pl.ds(ROWS + r, members, stride=tall), :]
    sum_ref[...] = jnp.zeros_like(sum_ref)


def exchange_block(
    block, stride, group, arrived_ref, bottom_ref, column_ref, sum_ref, table_ref, cells_ref
):
    members = table_ref.shape[1]
    size = arrived_ref.shape[0] // (cells_ref.shape[0] // group)

    def driver(v):
        return arrived_ref[pl.ds(block * size + v, group, stride=stride), :]

    leaf_temp = 35.0 * driver(1)
    column_ref[0] = 0.425 * 2000.0 * driver(0)
    column_ref[1] = arrhenius(65330.0, leaf_temp) * (0.2 + 0.8 * driver(2))
    column_ref[2] = arrhenius(43540.0, leaf_temp)
    column_ref[3] = 404.9 * arrhenius(79430.0, leaf_temp) * (
        1.0 + 210.0 / (278.4 * arrhenius(36380.0, leaf_temp))
    )
    column_ref[4] = 42.75 * arrhenius(37830.0, leaf_temp)
    leaf_area = 0.5 + 5.5 * driver(3)
    column_ref[5] = (-FLUX_SCALE / 0.5) * (0.05 + 0.55 * driver(4)) * (
        1.0 - jnp.exp(-0.5 * leaf_area)
    )
    column_ref[6] = driver(5)
    vref, jratio, rshare = table_ref[0], table_ref[1], table_ref[2]
    spread, places = [], []
    for i in range(group):
        shape = (members, LANES)

        def column(v):
            return jnp.broadcast_to(column_ref[v, i : i + 1, :], shape)

        cell = cells_ref[pl.ds(block * group + i, 1), :]
        cell_lane = jnp.broadcast_to(cell & 127, shape)
        cell_row = jnp.broadcast_to(cell >> 7, shape)
        bottom = lane_take(bottom_ref[0], cell_lane)
        for r in range(1, ROWS):
            bottom = jnp.where(cell_row == r, lane_take(bottom_ref[r], cell_lane), bottom)
        kind = column(6).astype(jnp.int32)
        rate = lane_take(vref, kind)
        vmax = rate * column(1)
        jmax = lane_take(jratio, kind) * rate * column(2)
        leaf = 0.7 * (400.0 + 100.0 * bottom)
        comp = column(4)
        absorbed = column(0)
        both = absorbed + jmax
        electron = (both - jnp.sqrt(both * both - 2.8 * absorbed * jmax)) * (1.0 / 1.4)
        excess = leaf - comp
        gross = jnp.minimum(
            vmax * excess / (leaf + column(3)),
            electron * excess / (4.0 * leaf + 8.0 * comp),
        )
        flux = column(5) * (gross - lane_take(rshare, kind) * vmax)
        high = flux.astype(jnp.bfloat16).astype(jnp.float32)
        low = flux - high
        spread.append(
            jnp.concatenate(
                [
                    jnp.where(cell_row == r, piece, 0.0)
                    for r in range(ROWS)
                    for piece in (high, low)
                ],
                axis=0,
            ).astype(jnp.bfloat16)
        )
        places.append(
            jnp.where(
                iota((LANES, LANES), 0) == jnp.broadcast_to(cell & 127, (LANES, LANES)),
                1.0,
                0.0,
            ).astype(jnp.bfloat16)
        )
    sum_ref[...] += lax.dot_general(
        jnp.concatenate(spread, axis=1),
        jnp.concatenate(places, axis=1),
        NT,
        preferred_element_type=jnp.float32,
    )


def advect_inside(
    last_lat, tracer_ref, courant_ref, tip_ref, west_ref, east_ref, partial_ref,
    weight_ref, ends_ref, rim_ref,
):
    levels = courant_ref.shape[0] // (2 * ROWS)
    fields = tracer_ref.shape[0] // ROWS - 2
    tall = levels * ROWS
    lane = iota((ROWS, LANES), 1)
    row = iota((ROWS, LANES), 0)
    is_last = lax.axis_index("lat") == last_lat
    packs = fields // 16
    place = lane & 7
    for j in range(packs + 1):
        at = slice(j * ROWS, (j + 1) * ROWS)
        ends_ref[at, :] = jnp.where(place < 3, west_ref[at, :], east_ref[at, :])
    wind_ends = ends_ref[packs * ROWS : (packs + 1) * ROWS, :]
    for level in range(levels):
        at = slice(level * ROWS, (level + 1) * ROWS)
        wind = courant_ref[at, :]
        outer = pltpu.roll(wind_ends, (LANES - 3 - 8 * level) % LANES, 1)
        behind = pltpu.roll(jnp.where(lane == LANES - 1, outer, wind), 1, 1)
        for k, w in enumerate(stencil(wind, behind)):
            weight_ref[k, at, :] = w
        wind = courant_ref[tall + level * ROWS : tall + (level + 1) * ROWS, :]
        wind = jnp.where(jnp.logical_and(row == ROWS - 1, is_last), 0.0, wind)
        outer = jnp.broadcast_to(
            tip_ref[level : level + 1, :], (ROWS, LANES)
        )
        behind = jnp.where(row == 0, outer, pltpu.roll(wind, 1, 0))
        for k, w in enumerate(stencil(wind, behind)):
            rim_ref[k, at, :] = w
            outside = jnp.logical_or(row + (k - 3) < 0, row + (k - 3) >= ROWS)
            inside = jnp.where(outside, 0.0, w)
            if k == 3:
                weight_ref[3, at, :] += 1.0 + inside
            else:
                weight_ref[7 + (k if k < 3 else k - 1), at, :] = inside

    def advance(j, carry):
        ends = ends_ref[pl.ds(pl.multiple_of(j * ROWS, ROWS), ROWS), :]
        for level in range(levels):
            at = slice(level * ROWS, (level + 1) * ROWS)
            weights = [weight_ref[k, at, :] for k in range(13)]
            for i in range(level, 16, levels):
                first = pl.multiple_of(j * 16 * ROWS + i * ROWS, ROWS)
                q = tracer_ref[pl.ds(first + ROWS, ROWS), :]
                outer = pltpu.roll(ends, (LANES - 3 - 8 * i) % LANES, 1)
                total = weights[3] * q
                for k in (1, 2, 3):
                    ahead = pltpu.roll(jnp.where(lane < k, outer, q), LANES - k, 1)
                    back = pltpu.roll(jnp.where(lane >= LANES - k, outer, q), k, 1)
                    total = total + (weights[3 + k] * ahead + weights[3 - k] * back)
                    total = total + (
                        weights[9 + k] * tracer_ref[pl.ds(first + ROWS + k, ROWS), :]
                        + weights[10 - k] * tracer_ref[pl.ds(first + ROWS - k, ROWS), :]
                    )
                partial_ref[pl.ds(first, ROWS), :] = total
        return carry

    lax.fori_loop(0, fields // 16, advance, 0)


def solve_weights(mixing_ref, solve_ref):
    levels = solve_ref.shape[1] // ROWS
    ratio = None
    for level in range(levels):
        at = slice(level * ROWS, (level + 1) * ROWS)
        zero = jnp.zeros((ROWS, LANES), jnp.float32)
        under = mixing_ref[level * ROWS - ROWS : level * ROWS, :] if level > 0 else zero
        over = mixing_ref[at, :] if level < levels - 1 else zero
        pivot = 1.0 + under + over
        if level > 0:
            pivot = pivot - under * ratio
        inverse = 1.0 / pivot
        ratio = over * inverse
        solve_ref[0, at, :] = inverse
        solve_ref[1, at, :] = under * inverse
        solve_ref[2, at, :] = ratio


def couple_kernel(
    lon, lat, stride,
    tracer_hbm, courant_hbm, mixing_hbm, forcing_hbm, plant_hbm, slot_hbm, params_hbm, cell_hbm,
    out_ref, surface_ref,
    tracer_ref, courant_ref, mixing_ref, forcing_ref, plant_ref, slot_ref, params_ref, cell_ref,
    below_ref, above_ref, partial_ref,
    values_ref, north_ref, south_ref, pack_ref, outgoing_ref, arrived_ref,
    bottom_ref, column_ref, sum_ref, table_ref, cells_ref, tip_ref, tip_out_ref, weight_ref, ends_ref,
    rim_ref, solve_ref, adv_ref,
    load_sem, round_sem, send_sem, recv_sem, up_send, up_recv, down_send, down_recv,
    side_send, side_recv,
    *sides_ref,
):
    my_lon, my_lat = lax.axis_index("lon"), lax.axis_index("lat")
    tiles = lon * lat
    size = outgoing_ref.shape[0] // tiles
    fields = partial_ref.shape[0] // ROWS
    levels = courant_ref.shape[0] // (2 * ROWS)
    tall = levels * ROWS
    members = fields // levels
    part = fields // GROUPS
    chunks = cells_ref.shape[0] // tiles
    has_above, has_below = my_lat < lat - 1, my_lat > 0
    east, west = {"lon": lax.rem(my_lon + 1, lon)}, {"lon": lax.rem(my_lon + lon - 1, lon)}
    beside = [east] if lon == 2 else [east, west]
    upper, lower = {"lat": lax.rem(my_lat + 1, lat)}, {"lat": lax.rem(my_lat + lat - 1, lat)}
    reach = lon // 2 + lat - 1

    def greet(sem):
        def signal(device):
            pl.semaphore_signal(
                sem, inc=1, device_id=device, device_id_type=pl.DeviceIdType.MESH
            )

        for device in beside:
            signal(device)

        @pl.when(has_above)
        def _():
            signal(upper)

        @pl.when(has_below)
        def _():
            signal(lower)

    neighbours = len(beside) + (my_lat + lat - 1) // lat + (2 * lat - 2 - my_lat) // lat

    def meet(sem):
        pl.semaphore_wait(sem, neighbours)

    barrier = pltpu.get_barrier_semaphore()
    greet(barrier)
    loads = [
        pltpu.make_async_copy(source, target, load_sem.at[i])
        for i, (source, target) in enumerate(
            [
                (tracer_hbm, tracer_ref.at[pl.ds(ROWS, fields * ROWS)]),
                (courant_hbm, courant_ref),
                (forcing_hbm, forcing_ref),
                (plant_hbm, plant_ref),
                (slot_hbm, slot_ref),
                (params_hbm, params_ref),
                (cell_hbm, cell_ref),
                (mixing_hbm, mixing_ref),
            ]
        )
    ]
    for load in loads:
        load.start()
    zero_tile = jnp.zeros((ROWS, LANES), jnp.float32)
    tracer_ref[0:ROWS, :] = zero_tile
    tracer_ref[ROWS + fields * ROWS : 2 * ROWS + fields * ROWS, :] = zero_tile
    adv_ref[...] = jnp.zeros_like(adv_ref)
    loads[0].wait()
    loads[1].wait()
    pack_rows(tracer_ref, courant_ref, north_ref, south_ref, tip_out_ref)
    pack_lanes(tracer_ref, courant_ref, pack_ref)
    meet(barrier)
    if reach > 1:
        greet(round_sem.at[0])

    def remote(source, target, send, recv, device):
        return pltpu.make_async_remote_copy(
            src_ref=source, dst_ref=target, send_sem=send, recv_sem=recv,
            device_id=device, device_id_type=pl.DeviceIdType.MESH,
        )

    def up(g):
        span = pl.ds(g * 3 * part, 3 * part)
        return remote(north_ref.at[span], below_ref.at[span], up_send.at[g], up_recv.at[g], upper)

    def down(g):
        span = pl.ds(g * 3 * part, 3 * part)
        return remote(
            south_ref.at[span], above_ref.at[span], down_send.at[g], down_recv.at[g], lower
        )

    tip = remote(tip_out_ref, tip_ref, side_send.at[2], side_recv.at[2], upper)
    sides = [
        remote(pack_ref, sides_ref[i], side_send.at[i], side_recv.at[i], device)
        for i, device in enumerate(beside)
    ]

    def start_halo(first, last):
        @pl.when(has_above)
        def _():
            for g in range(first, last):
                up(g).start()

        @pl.when(has_below)
        def _():
            for g in range(first, last):
                down(g).start()

    def peer(i):
        dx, dy = i % lon, i // lon
        return lax.rem(my_lon + dx, lon), flip(my_lat, dy, lat)

    mine = pl.ds(pl.multiple_of((my_lon * lat + my_lat) * size, size), size)

    def move(i):
        x, y = peer(i)
        theirs = pl.ds(pl.multiple_of((x * lat + y) * size, size), size)
        return remote(
            outgoing_ref.at[theirs], arrived_ref.at[mine], send_sem.at[i], recv_sem.at[i],
            {"lon": x, "lat": y},
        )

    def start_moves(distance):
        for i in range(1, tiles):
            dx, dy = i % lon, i // lon
            if min(dx, lon - dx) + dy == distance:
                move(i).start()

    @pl.when(has_above)
    def _():
        tip.start()

    for side in sides:
        side.start()
    early = 3
    start_halo(0, early)
    for load in loads[2:]:
        load.wait()
    pack_columns(stride, forcing_ref, plant_ref, slot_ref, outgoing_ref, values_ref)
    start_moves(1)
    arrived_ref[mine, :] = outgoing_ref[mine, :]
    prepare_exchange(tracer_ref, params_ref, cell_ref, bottom_ref, sum_ref, table_ref, cells_ref)
    for distance in range(2, reach + 1):
        meet(round_sem.at[distance - 2])
        if distance < reach:
            greet(round_sem.at[distance - 1])
        start_moves(distance)
        if distance == 2:
            solve_weights(mixing_ref, solve_ref)
    start_halo(early, GROUPS)

    @pl.when(my_lat == 0)
    def _():
        below_ref[...] = jnp.zeros_like(below_ref)
        tip_ref[...] = jnp.zeros_like(tip_ref)

    @pl.when(my_lat == lat - 1)
    def _():
        above_ref[...] = jnp.zeros_like(above_ref)

    for side in sides:
        side.wait()

    @pl.when(has_above)
    def _():
        tip.wait_send()

    @pl.when(has_below)
    def _():
        tip.wait_recv()

    advect_inside(
        lat - 1, tracer_ref, courant_ref, tip_ref, sides_ref[0], sides_ref[-1], partial_ref,
        weight_ref, ends_ref, rim_ref,
    )

    def exchange(i, carry):
        @pl.when(i > 0)
        def _():
            move(i).wait_recv()

        source = lax.rem(my_lon + lon - i % lon, lon) * lat + flip(my_lat, i // lon, lat)
        exchange_block(
            source, stride, chunks, arrived_ref, bottom_ref, column_ref, sum_ref, table_ref,
            cells_ref,
        )
        return carry

    lax.fori_loop(0, tiles, exchange, 0)
    for r in range(ROWS):
        at = 2 * members * r
        surface_ref[pl.ds(r, members, stride=ROWS), :] = (
            sum_ref[at : at + members, :] + sum_ref[at + members : at + 2 * members, :]
        )

    def rim(k, r):
        return rim_ref[k, pl.ds(r, levels, stride=ROWS), :]

    below = [[(h, rim(h - r, r)) for h in range(r, 3)] for r in range(3)]
    above = [[(h, rim(h + 3 + d, ROWS - d)) for h in range(0, 4 - d)] for d in range(1, 4)]
    span = members // GROUPS

    def finish(g, carry):
        @pl.when(has_below)
        def _():
            up(g).wait_recv()

        @pl.when(has_above)
        def _():
            down(g).wait_recv()

        for u in range(span):
            near = adv_ref.at[u]
            first = pl.multiple_of(g * 3 * part + u * levels, levels)
            for r in range(3):
                near[pl.ds(r, levels, stride=ROWS), :] = sum(
                    w * below_ref[pl.ds(first + h * part, levels), :] for h, w in below[r]
                )
            for d in range(1, 4):
                near[pl.ds(ROWS - d, levels, stride=ROWS), :] = sum(
                    w * above_ref[pl.ds(first + h * part, levels), :] for h, w in above[d - 1]
                )
        for u in range(span):
            m = g * span + u
            base = pl.multiple_of(m * tall, tall)
            value, values = None, []
            for level in range(levels):
                at = slice(level * ROWS, (level + 1) * ROWS)
                total = adv_ref[u, at, :] + partial_ref[pl.ds(base + level * ROWS, ROWS), :]
                if level == 0:
                    total = total + surface_ref[pl.ds(pl.multiple_of(m * ROWS, ROWS), ROWS), :]
                    value = total * solve_ref[0, at, :]
                else:
                    value = total * solve_ref[0, at, :] + solve_ref[1, at, :] * value
                values.append(value)
            for level in range(levels - 1, -1, -1):
                at = slice(level * ROWS, (level + 1) * ROWS)
                if level < levels - 1:
                    value = values[level] + solve_ref[2, at, :] * value
                out_ref[pl.ds(base + level * ROWS, ROWS), :] = value
        return carry

    lax.fori_loop(0, GROUPS, finish, 0)
    for i in range(1, tiles):
        move(i).wait_send()

    @pl.when(has_above)
    def _():
        for g in range(GROUPS):
            up(g).wait_send()

    @pl.when(has_below)
    def _():
        for g in range(GROUPS):
            down(g).wait_send()


def store_kernel(tracer_ref, surface_ref, tracer_out, surface_out, sem):
    copies = [
        pltpu.make_async_copy(tracer_ref, tracer_out, sem.at[0]),
        pltpu.make_async_copy(surface_ref, surface_out, sem.at[1]),
    ]
    for copy in copies:
        copy.start()
    for copy in copies:
        copy.wait()


def per_device(tracer, courant, mixing, forcing, plant_type, land_params, send_slot, recv_cell):
    members, levels, rows, lanes = tracer.shape
    fields = members * levels
    lon, lat = lax.axis_size("lon"), lax.axis_size("lat")
    tiles = lon * lat
    slots = recv_cell.shape[1]
    padded = -(-slots // LANES) * LANES
    if padded != slots:
        send_slot = jnp.where(
            send_slot >= 0, send_slot // slots * padded + send_slot % slots, -1
        )
        recv_cell = jnp.pad(
            recv_cell, ((0, 0), (0, padded - slots)), constant_values=rows * lanes
        )
    chunks = padded // LANES
    stride = 6 if 6 * chunks % ROWS == 0 else ROWS
    f32 = functools.partial(jax.ShapeDtypeStruct, dtype=jnp.float32)
    vmem = functools.partial(pltpu.VMEM, dtype=jnp.float32)
    integers = functools.partial(pltpu.VMEM, dtype=jnp.int32)
    dma = pltpu.SemaphoreType.DMA
    packs = (fields // 16 + 1) * ROWS
    tall = levels * rows
    columns = forcing.shape[1]
    side_count = 1 if lon == 2 else 2
    anywhere = pl.BlockSpec(memory_space=pltpu.HBM)
    tracer_next, surface = pl.pallas_call(
        functools.partial(couple_kernel, lon, lat, stride),
        out_shape=(f32((fields * rows, lanes)), f32((members * rows, lanes))),
        in_specs=[anywhere] * 8,
        out_specs=(pl.BlockSpec(memory_space=pltpu.VMEM),) * 2,
        scratch_shapes=[
            vmem(((fields + 2) * rows, lanes)),
            vmem((2 * tall, lanes)),
            vmem(((levels - 1) * rows, lanes)),
            vmem(forcing.shape),
            integers((1, columns)),
            integers((1, columns)),
            vmem((3, land_params.shape[2], members)),
            integers(recv_cell.shape),
            vmem((3 * fields, lanes)),
            vmem((3 * fields, lanes)),
            vmem((fields * rows, lanes)),
            vmem((stride * chunks, columns)),
            vmem((3 * fields, lanes)),
            vmem((3 * fields, lanes)),
            vmem((packs, lanes)),
            vmem((tiles * chunks * stride, lanes)),
            vmem((tiles * chunks * stride, lanes)),
            vmem((ROWS, members, lanes)),
            vmem((7, chunks, lanes)),
            vmem((2 * members * ROWS, lanes)),
            vmem((3, members, lanes)),
            integers((tiles * chunks, lanes)),
            vmem((levels, lanes)),
            vmem((levels, lanes)),
            vmem((13, tall, lanes)),
            vmem((packs, lanes)),
            vmem((7, tall, lanes)),
            vmem((3, tall, lanes)),
            vmem((members // GROUPS, tall, lanes)),
            dma((8,)),
            pltpu.SemaphoreType.REGULAR((lon // 2 + lat - 1,)),
            dma((tiles,)),
            dma((tiles,)),
            dma((GROUPS,)),
            dma((GROUPS,)),
            dma((GROUPS,)),
            dma((GROUPS,)),
            dma((3,)),
            dma((3,)),
            *[vmem((packs, lanes))] * side_count,
        ],
        compiler_params=pltpu.CompilerParams(
            collective_id=0, has_side_effects=True, vmem_limit_bytes=16 << 20
        ),
        name="couple",
    )(
        *[
            pltpu.with_memory_space_constraint(operand, pltpu.HBM)
            for operand in (
                tracer.reshape(fields * rows, lanes), courant.reshape(2 * tall, lanes),
                mixing.reshape((levels - 1) * rows, lanes), forcing, plant_type[None, :],
                send_slot[None, :], land_params.swapaxes(1, 2), recv_cell,
            )
        ]
    )
    here = pl.BlockSpec(memory_space=pltpu.VMEM)
    tracer_next, surface = pl.pallas_call(
        store_kernel,
        out_shape=(f32((fields * rows, lanes)), f32((members * rows, lanes))),
        in_specs=[here, here],
        out_specs=(anywhere, anywhere),
        scratch_shapes=[dma((2,))],
        compiler_params=pltpu.CompilerParams(vmem_limit_bytes=16 << 20),
        name="store",
    )(tracer_next, surface)
    return tracer_next.reshape(tracer.shape), surface.reshape(members, rows, lanes)


def solution(mesh):
    in_specs = (
        P("mem", None, "lat", "lon"),
        P(None, None, "lat", "lon"),
        P(None, "lat", "lon"),
        P(None, ("lon", "lat")),
        P(("lon", "lat")),
        P(None, "mem", None),
        P(("lon", "lat")),
        P(("lon", "lat"), None),
    )
    out_specs = (P("mem", None, "lat", "lon"), P("mem", "lat", "lon"))
    return jax.shard_map(
        per_device, mesh=mesh, in_specs=in_specs, out_specs=out_specs, check_vma=False
    )
```
